512 devices in a mesh: sec: 16 (over y, x), tile: 32 (over z, core).
Axes of the slice: x: 4, y: 4, z: 16, core: 2. Of those that a mesh axis runs over, the one named last changes fastest.
Arguments:
- beams: float32 [16, 2, 512, 2048], P('sec', None, 'tile'), may hold values from -6 to 6
- medium: float32 [16, 512, 2048], P('sec', 'tile'), may hold values from -0.3 to 0.3
Outputs:
- exit_fields: float32 [16, 2, 512, 2048], P('sec', None, 'tile')
The draws below stay inside these ranges and needn't reach their ends.
All inputs are finite; a program needn't handle non-finite values.
Results may differ from the reference program's by a relative error of at most 0.00002.
Values sent between devices are 32-bit elements; how exact they have to be, the bound alone decides.
A program may use at most 64 MiB of HBM per device.

```python
import jax
import jax.numpy as jnp
from jax import lax

COLS = 2048
STEPS = 1
ROWS = 512
SECTIONS = 16
REALIZATIONS = 16


def steps_of(key, shape, pieces, smallest, high):
    def one(dim, shards_of):
        draws = jax.random.uniform(jax.random.fold_in(jax.random.fold_in(key, 6), dim), (shards_of,), jnp.float32, smallest / len(pieces), high / len(pieces))
        return jnp.repeat(jnp.exp(draws), shape[dim] // shards_of).reshape((-1,) + (1,) * (len(shape) - dim - 1))

    level = one(*pieces[0])
    for cut in pieces[1:]:
        level = level * one(*cut)
    return level


def noise(stream_key, shape, deviation, reach, pieces=(), kind=jnp.bfloat16):
    values = jax.random.normal(stream_key, shape, jnp.float32) * deviation
    if len(pieces) > 0:
        values = steps_of(stream_key, shape, pieces, -0.22, 0.18) * values
    return jnp.clip(values, min=-reach, max=reach).astype(kind)


def setup_inputs(seed: int = 0) -> dict:
    streams_of = jax.random.split(jax.random.key(seed), 3)
    return {
        "beams": noise(streams_of[0], (REALIZATIONS, 2, ROWS, COLS), 1.0, 6.0, ((0, 16), (2, 32)), jnp.float32),
        "medium": jnp.clip(jax.random.uniform(streams_of[1], (SECTIONS, ROWS, COLS), jnp.float32, -0.3, 0.3) * steps_of(streams_of[1], (SECTIONS, ROWS, COLS), ((0, 16), (1, 32)), -0.4, 0.0), -0.3, 0.3),
    }


diffract_coef = 0.5
step_length = 0.65


def laplace(envelope):
    pads = [(0, 0)] * (envelope.ndim - 2) + [(1, 1), (1, 1)]
    padded = jnp.pad(envelope, pads)
    return padded[..., :-2, 1:-1] + padded[..., 2:, 1:-1] + padded[..., 1:-1, :-2] + padded[..., 1:-1, 2:] - 4.0 * envelope


def derivative(envelope, medium_ext, inside):
    masked = envelope * inside
    forcing = diffract_coef * laplace(masked) + medium_ext * masked
    return jnp.stack([-forcing[..., 1, :, :], forcing[..., 0, :, :]], axis=-3)


def advance(envelope, medium_ext, inside):
    half_length = 0.5 * step_length
    slope_one = derivative(envelope, medium_ext, inside)
    slope_two = derivative(envelope + half_length * slope_one, medium_ext, inside)
    slope_three = derivative(envelope + half_length * slope_two, medium_ext, inside)
    slope_four = derivative(envelope + step_length * slope_three, medium_ext, inside)
    return envelope + (step_length / 6.0) * (slope_one + 2.0 * slope_two + 2.0 * slope_three + slope_four)


def reference(beams, medium):
    def per_beam(envelope):
        def section(state_field, slab_piece):
            for repeat in range(STEPS):
                state_field = advance(state_field, slab_piece, 1.0)
            return state_field, None

        final_field, unused = lax.scan(section, envelope, medium)
        return final_field

    return lax.map(per_beam, beams)
```

```python
import functools

import jax
import jax.numpy as jnp
from jax import lax
from jax.experimental import pallas as pl
from jax.experimental.pallas import tpu as pltpu
from jax.sharding import PartitionSpec as P

MESH = pl.DeviceIdType.MESH
STEP = 0.65
DIFFRACT = 0.5
SCALES = tuple(DIFFRACT * STEP / d for d in (4.0, 3.0, 2.0, 1.0))
GROUP = 4
PANELS = 16
LANES = 128
UNROLL = 4


def swap_bits(tiles):
    lane = lax.broadcasted_iota(jnp.int32, tiles[0].shape, len(tiles[0].shape) - 1)
    axis = len(tiles[0].shape) - 1
    tiles = list(tiles)
    for bit in range(4):
        low = (lane & (1 << bit)) == 0
        for i in range(PANELS):
            if i & (1 << bit):
                continue
            j = i | (1 << bit)
            x, y = tiles[i], tiles[j]
            tiles[i] = jnp.where(low, x, pltpu.roll(y, 1 << bit, axis))
            tiles[j] = jnp.where(low, pltpu.roll(x, LANES - (1 << bit), axis), y)
    return tiles


def kernel(tiles, secs, beams, medium, out, field, work, index, scale, m_send, m_recv, h_send, h_recv, f_send, f_recv):
    rows = medium.shape[1]
    ext = 3 * rows
    pad = 8
    me = lax.axis_index("sec")
    t = lax.axis_index("tile")
    odd = lax.rem(t, 2)
    y, x = lax.div(me, 4), lax.rem(me, 4)
    a = x * (1 - odd) + y * odd
    b = y * (1 - odd) + x * odd

    def sid(da, db):
        return lax.rem(a + da, 4) * (1 + 3 * odd) + lax.rem(b + db, 4) * (4 - 3 * odd)

    has_up = t > 0
    has_down = t < tiles - 1

    barrier = pltpu.get_barrier_semaphore()
    for peer in (sid(1, 0), sid(3, 0), sid(0, 1), sid(0, 3)):
        pl.semaphore_signal(barrier, inc=1, device_id=(peer, t), device_id_type=MESH)

    @pl.when(has_up)
    def _():
        pl.semaphore_signal(barrier, inc=1, device_id=(me, t - 1), device_id_type=MESH)

    @pl.when(has_down)
    def _():
        pl.semaphore_signal(barrier, inc=1, device_id=(me, t + 1), device_id_type=MESH)

    for r in range(0, rows, 8):
        m = [2.0 * medium[0, r : r + 8, k * LANES : (k + 1) * LANES] - 4.0 for k in range(PANELS)]
        for k, v in enumerate(swap_bits(m)):
            index[me, k, rows + r : rows + r + 8, :] = v
    for p in range(2):
        for r in range(0, rows, 8):
            f = [beams[0, p, r : r + 8, k * LANES : (k + 1) * LANES] for k in range(PANELS)]
            for k, v in enumerate(swap_bits(f)):
                field[0, p, k + 1, pad + rows + r : pad + rows + r + 8, :] = v

    zero = jnp.zeros((8, LANES), jnp.float32)

    @pl.loop(0, PANELS + 2)
    def _(k):
        for i in range(2):
            for p in range(2):
                for r in (0, pad + ext):
                    field[i, p, k, r : r + 8, :] = zero
                    work[i, p, k, r : r + 8, :] = zero

    def clear(first):
        @pl.loop(0, PANELS + 2)
        def _(k):
            for i in range(2):
                for p in range(2):
                    for r in range(0, rows, 8):
                        field[i, p, k, pad + first + r : pad + first + r + 8, :] = zero

        @pl.loop(0, secs)
        def _(s):
            for k in range(PANELS):
                for r in range(0, rows, 8):
                    index[s, k, first + r : first + r + 8, :] = zero

    @pl.when(jnp.logical_not(has_up))
    def _():
        clear(0)

    @pl.when(jnp.logical_not(has_down))
    def _():
        clear(2 * rows)

    for r in range(0, ext, 8):
        place = lax.broadcasted_iota(jnp.int32, (8, LANES), 0) + (t * rows + r - rows)
        inside = jnp.logical_and(place >= 0, place < tiles * rows)
        for i, c in enumerate(SCALES):
            scale[i, r : r + 8, :] = jnp.where(inside, jnp.float32(c), jnp.float32(0.0))

    up_edge = (pad + rows, pad + 2 * rows)

    def field_copy(buf, side):
        mine = field.at[buf, :, 1 : PANELS + 1, pad + rows : pad + 2 * rows, :]
        first = pad + (2 * rows if side == 0 else 0)
        theirs = field.at[buf, :, 1 : PANELS + 1, first : first + rows, :]
        return pltpu.make_async_remote_copy(
            src_ref=mine, dst_ref=theirs, send_sem=f_send.at[buf, side], recv_sem=f_recv.at[buf, side],
            device_id=(me, t - 1 if side == 0 else t + 1), device_id_type=MESH)

    def index_copy(s, depth, side):
        first = rows if side == 0 else 2 * rows - depth
        there = 2 * rows if side == 0 else rows - depth
        return pltpu.make_async_remote_copy(
            src_ref=index.at[s, :, first : first + depth, :], dst_ref=index.at[s, :, there : there + depth, :],
            send_sem=h_send.at[s, side], recv_sem=h_recv.at[s, side],
            device_id=(me, t - 1 if side == 0 else t + 1), device_id_type=MESH)

    def both(make, act):
        @pl.when(has_up)
        def _():
            act(make(0))

        @pl.when(has_down)
        def _():
            act(make(1))

    def both_in(make, act):
        @pl.when(has_down)
        def _():
            act(make(0))

        @pl.when(has_up)
        def _():
            act(make(1))

    pl.semaphore_wait(barrier, 4 + has_up.astype(jnp.int32) + has_down.astype(jnp.int32))

    both(lambda side: field_copy(0, side), lambda c: c.start())

    sends = []
    halves = (pl.ds(0, PANELS // 2), pl.ds(PANELS // 2, PANELS // 2))
    every = pl.ds(0, PANELS)

    def send(s, part, peer):
        ref = index.at[s, part, rows : 2 * rows, :]
        copy = pltpu.make_async_remote_copy(
            src_ref=ref, dst_ref=ref, send_sem=m_send.at[len(sends)], recv_sem=m_recv.at[s],
            device_id=(peer, t), device_id_type=MESH)
        copy.start()
        sends.append(copy)

    def arrived(s):
        ref = index.at[s, :, rows : 2 * rows, :]
        pltpu.make_async_remote_copy(
            src_ref=ref, dst_ref=ref, send_sem=m_send.at[0], recv_sem=m_recv.at[s],
            device_id=(me, t), device_id_type=MESH).wait_recv()

    send(me, every, sid(1, 0))
    send(me, every, sid(3, 0))
    send(me, every, sid(0, 1))
    send(me, every, sid(0, 3))
    arrived(sid(3, 0))
    send(sid(3, 0), halves[0], sid(1, 0))
    arrived(sid(1, 0))
    send(sid(1, 0), halves[1], sid(3, 0))
    for da in (3, 1):
        send(sid(da, 0), every, sid(0, 1))
        send(sid(da, 0), every, sid(0, 3))
    arrived(sid(2, 0))
    send(sid(2, 0), every, sid(0, 1))
    send(sid(2, 0), every, sid(0, 3))
    for da in (0, 3, 1, 2):
        arrived(sid(da, 3))
        send(sid(da, 3), halves[0], sid(0, 1))
        arrived(sid(da, 1))
        send(sid(da, 1), halves[1], sid(0, 3))
    for da in (0, 3, 1, 2):
        arrived(sid(da, 2))

    def depth_of(s):
        return rows if s % GROUP < GROUP // 2 else rows // 2

    for s in range(secs):
        both(lambda side, s=s: index_copy(s, depth_of(s), side), lambda c: c.start())

    lane = lax.broadcasted_iota(jnp.int32, (8, LANES), 1)

    def ghosts(ref, first, last):
        for p in range(2):
            for blk in range(first, last):
                r = pad + 8 * blk
                v = ref[p, PANELS, r : r + 8, :]
                left = jnp.where(lane < 16, pltpu.roll(v, 17, 1), pltpu.roll(v, 16, 1))
                ref[p, 0, r : r + 8, :] = jnp.where(lane == 0, 0.0, left)
                v = ref[p, 1, r : r + 8, :]
                right = jnp.where(lane >= LANES - 16, pltpu.roll(v, LANES - 17, 1), pltpu.roll(v, LANES - 16, 1))
                ref[p, PANELS + 1, r : r + 8, :] = jnp.where(lane == LANES - 1, 0.0, right)

    def stage(src, dst, base, s, i, first, last):
        weights = [scale[i, 8 * blk : 8 * blk + 8, :] for blk in range(first, last)]

        @pl.loop(0, PANELS // UNROLL)
        def _(step):
            k0 = step * UNROLL
            for blk in range(first, last):
                r = pad + 8 * blk
                w = weights[blk - first]
                mid = [[src[p, k0 + q, r : r + 8, :] for q in range(UNROLL + 2)] for p in range(2)]
                for u in range(UNROLL):
                    m = index[s, k0 + u, 8 * blk : 8 * blk + 8, :]
                    drive = []
                    for p in range(2):
                        rowsum = src[p, k0 + u + 1, r - 1 : r + 7, :] + src[p, k0 + u + 1, r + 1 : r + 9, :]
                        drive.append(((mid[p][u] + mid[p][u + 2]) + rowsum + m * mid[p][u + 1]) * w)
                    dst[0, k0 + u + 1, r : r + 8, :] = base[0, k0 + u + 1, r : r + 8, :] - drive[1]
                    dst[1, k0 + u + 1, r : r + 8, :] = base[1, k0 + u + 1, r : r + 8, :] + drive[0]

        ghosts(dst, first, last)

    groups = secs // GROUP

    @pl.loop(0, groups)
    def _(g):
        now, later = lax.rem(g, 2), lax.rem(g + 1, 2)
        cur, nxt = field.at[now], field.at[later]
        both_in(lambda side: field_copy(now, side), lambda c: c.wait_recv())
        both(lambda side: field_copy(now, side), lambda c: c.wait_send())
        for j in range(GROUP):
            both_in(lambda side, j=j: index_copy(g * GROUP + j, depth_of(j), side), lambda c: c.wait_recv())
        ghosts(cur, 0, ext // 8)
        for j in range(GROUP):
            s = g * GROUP + j
            for i in range(4):
                n = 4 * j + i + 1
                first, last = n // 8, -(-(ext - n) // 8)
                src = cur if i == 0 else work.at[(i + 1) % 2]
                dst = work.at[i % 2] if i < 3 else (cur if j < GROUP - 1 else nxt)
                stage(src, dst, cur, s, i, first, last)

        @pl.when(g < groups - 1)
        def _():
            both(lambda side: field_copy(later, side), lambda c: c.start())

    final = field.at[groups % 2]
    for p in range(2):
        for r in range(0, rows, 8):
            f = [final[p, k + 1, pad + rows + r : pad + rows + r + 8, :] for k in range(PANELS)]
            for k, v in enumerate(swap_bits(f)):
                out[0, p, r : r + 8, k * LANES : (k + 1) * LANES] = v

    for copy in sends:
        copy.wait_send()
    for s in range(secs):
        both(lambda side, s=s: index_copy(s, depth_of(s), side), lambda c: c.wait_send())


def per_device(tiles, secs, beams, medium):
    rows = medium.shape[1]
    vmem = pl.BlockSpec(memory_space=pltpu.VMEM)
    return pl.pallas_call(
        functools.partial(kernel, tiles, secs),
        out_shape=jax.ShapeDtypeStruct(beams.shape, jnp.float32),
        in_specs=[vmem, vmem],
        out_specs=vmem,
        scratch_shapes=[
            pltpu.VMEM((2, 2, PANELS + 2, 3 * rows + 16, LANES), jnp.float32),
            pltpu.VMEM((2, 2, PANELS + 2, 3 * rows + 16, LANES), jnp.float32),
            pltpu.VMEM((secs, PANELS, 3 * rows, LANES), jnp.float32),
            pltpu.VMEM((4, 3 * rows, LANES), jnp.float32),
            pltpu.SemaphoreType.DMA((20,)),
            pltpu.SemaphoreType.DMA((secs,)),
            pltpu.SemaphoreType.DMA((secs, 2)),
            pltpu.SemaphoreType.DMA((secs, 2)),
            pltpu.SemaphoreType.DMA((2, 2)),
            pltpu.SemaphoreType.DMA((2, 2)),
        ],
        compiler_params=pltpu.CompilerParams(collective_id=0, has_side_effects=True),
        name="propagate",
    )(beams, medium)


def solution(mesh):
    placed = (P("sec", None, "tile", None), P("sec", "tile", None))
    return jax.shard_map(
        functools.partial(per_device, mesh.shape["tile"], mesh.shape["sec"]),
        mesh=mesh,
        in_specs=placed,
        out_specs=P("sec", None, "tile", None),
        check_vma=False,
    )
```

```python
import functools

import jax
import jax.numpy as jnp
from jax import lax
from jax.experimental import pallas as pl
from jax.experimental.pallas import tpu as pltpu
from jax.sharding import PartitionSpec as P

MESH = pl.DeviceIdType.MESH
STEP = 0.65
DIFFRACT = 0.5
SCALES = tuple(DIFFRACT * STEP / d for d in (4.0, 3.0, 2.0, 1.0))
GROUP = 4
PANELS = 16
LANES = 128
UNROLL = 4


def swap_bits(tiles):
    lane = lax.broadcasted_iota(jnp.int32, tiles[0].shape, len(tiles[0].shape) - 1)
    axis = len(tiles[0].shape) - 1
    tiles = list(tiles)
    for bit in range(4):
        low = (lane & (1 << bit)) == 0
        for i in range(PANELS):
            if i & (1 << bit):
                continue
            j = i | (1 << bit)
            x, y = tiles[i], tiles[j]
            tiles[i] = jnp.where(low, x, pltpu.roll(y, 1 << bit, axis))
            tiles[j] = jnp.where(low, pltpu.roll(x, LANES - (1 << bit), axis), y)
    return tiles


def kernel(tiles, secs, beams, medium, out, field, work, index, scale, m_send, m_recv, h_send, h_recv, f_send, f_recv):
    rows = medium.shape[1]
    ext = 3 * rows
    pad = 8
    me = lax.axis_index("sec")
    t = lax.axis_index("tile")
    odd = lax.rem(t, 2)
    y, x = lax.div(me, 4), lax.rem(me, 4)
    a = x * (1 - odd) + y * odd
    b = y * (1 - odd) + x * odd

    def sid(da, db):
        return lax.rem(a + da, 4) * (1 + 3 * odd) + lax.rem(b + db, 4) * (4 - 3 * odd)

    has_up = t > 0
    has_down = t < tiles - 1

    barrier = pltpu.get_barrier_semaphore()
    for peer in (sid(1, 0), sid(3, 0), sid(0, 1), sid(0, 3)):
        pl.semaphore_signal(barrier, inc=1, device_id=(peer, t), device_id_type=MESH)

    @pl.when(has_up)
    def _():
        pl.semaphore_signal(barrier, inc=1, device_id=(me, t - 1), device_id_type=MESH)

    @pl.when(has_down)
    def _():
        pl.semaphore_signal(barrier, inc=1, device_id=(me, t + 1), device_id_type=MESH)

    def field_copy(buf, side):
        mine = field.at[buf, :, 1 : PANELS + 1, pad + rows : pad + 2 * rows, :]
        first = pad + (2 * rows if side == 0 else 0)
        theirs = field.at[buf, :, 1 : PANELS + 1, first : first + rows, :]
        return pltpu.make_async_remote_copy(
            src_ref=mine, dst_ref=theirs, send_sem=f_send.at[buf, side], recv_sem=f_recv.at[buf, side],
            device_id=(me, t - 1 if side == 0 else t + 1), device_id_type=MESH)

    def index_copy(s, depth, side):
        first = rows if side == 0 else 2 * rows - depth
        there = 2 * rows if side == 0 else rows - depth
        return pltpu.make_async_remote_copy(
            src_ref=index.at[s, :, first : first + depth, :], dst_ref=index.at[s, :, there : there + depth, :],
            send_sem=h_send.at[s, side], recv_sem=h_recv.at[s, side],
            device_id=(me, t - 1 if side == 0 else t + 1), device_id_type=MESH)

    def both(make, act):
        @pl.when(has_up)
        def _():
            act(make(0))

        @pl.when(has_down)
        def _():
            act(make(1))

    def both_in(make, act):
        @pl.when(has_down)
        def _():
            act(make(0))

        @pl.when(has_up)
        def _():
            act(make(1))

    def depth_of(j):
        return rows - 4 * j

    sends = []
    halves = (pl.ds(0, PANELS // 2), pl.ds(PANELS // 2, PANELS // 2))
    every = pl.ds(0, PANELS)

    def send(s, part, peer):
        ref = index.at[s, part, rows : 2 * rows, :]
        copy = pltpu.make_async_remote_copy(
            src_ref=ref, dst_ref=ref, send_sem=m_send.at[len(sends)], recv_sem=m_recv.at[s],
            device_id=(peer, t), device_id_type=MESH)
        copy.start()
        sends.append(copy)

    def edges(s):
        for j in range(GROUP):
            @pl.when(lax.rem(s, GROUP) == j)
            def _():
                both(lambda side: index_copy(s, depth_of(j), side), lambda c: c.start())

    def arrived(s):
        ref = index.at[s, :, rows : 2 * rows, :]
        pltpu.make_async_remote_copy(
            src_ref=ref, dst_ref=ref, send_sem=m_send.at[0], recv_sem=m_recv.at[s],
            device_id=(me, t), device_id_type=MESH).wait_recv()

    for r in range(0, rows, 8):
        m = [2.0 * medium[0, r : r + 8, k * LANES : (k + 1) * LANES] - 4.0 for k in range(PANELS)]
        for k, v in enumerate(swap_bits(m)):
            index[me, k, rows + r : rows + r + 8, :] = v
    pl.semaphore_wait(barrier, 4 + has_up.astype(jnp.int32) + has_down.astype(jnp.int32))
    send(me, every, sid(1, 0))
    send(me, every, sid(3, 0))
    send(me, every, sid(0, 1))
    send(me, every, sid(0, 3))
    for p in range(2):
        for r in range(0, rows, 8):
            f = [beams[0, p, r : r + 8, k * LANES : (k + 1) * LANES] for k in range(PANELS)]
            for k, v in enumerate(swap_bits(f)):
                field[0, p, k + 1, pad + rows + r : pad + rows + r + 8, :] = v

    both(lambda side: field_copy(0, side), lambda c: c.start())
    lane = lax.broadcasted_iota(jnp.int32, (8, LANES), 1)

    def before_first(v):
        left = jnp.where(lane < 16, pltpu.roll(v, 17, 1), pltpu.roll(v, 16, 1))
        return jnp.where(lane == 0, 0.0, left)

    def after_last(v):
        right = jnp.where(lane >= LANES - 16, pltpu.roll(v, LANES - 17, 1), pltpu.roll(v, LANES - 16, 1))
        return jnp.where(lane == LANES - 1, 0.0, right)

    def ghosts(ref, blocks):
        for blk in blocks:
            for p in range(2):
                r = pad + 8 * blk
                ref[p, 0, r : r + 8, :] = before_first(ref[p, PANELS, r : r + 8, :])
                ref[p, PANELS + 1, r : r + 8, :] = after_last(ref[p, 1, r : r + 8, :])

    def stage(src, dst, base, s, i, first, last):
        for k0 in (PANELS - UNROLL,) + tuple(range(0, PANELS - UNROLL, UNROLL)):
            for blk in range(first, last):
                r = pad + 8 * blk
                w = scale[i, 8 * blk : 8 * blk + 8, :]
                mid = [[src[p, k0 + q, r : r + 8, :] for q in range(UNROLL + 2)] for p in range(2)]
                for u in range(UNROLL):
                    k = k0 + u
                    m = index[s, k, 8 * blk : 8 * blk + 8, :]
                    drive = []
                    for p in range(2):
                        rowsum = src[p, k + 1, r - 1 : r + 7, :] + src[p, k + 1, r + 1 : r + 9, :]
                        drive.append(((mid[p][u] + mid[p][u + 2]) + rowsum + m * mid[p][u + 1]) * w)
                    new = (base[0, k + 1, r : r + 8, :] - drive[1], base[1, k + 1, r : r + 8, :] + drive[0])
                    for p in range(2):
                        dst[p, k + 1, r : r + 8, :] = new[p]
                        if k == 0:
                            dst[p, PANELS + 1, r : r + 8, :] = after_last(new[p])
                        if k == PANELS - 1:
                            dst[p, 0, r : r + 8, :] = before_first(new[p])

    ghosts(field.at[0], range(rows // 8, 2 * rows // 8))
    zero = jnp.zeros((8, LANES), jnp.float32)

    @pl.loop(0, PANELS + 2)
    def _(k):
        for i in range(2):
            for p in range(2):
                for r in (0, pad + ext):
                    field[i, p, k, r : r + 8, :] = zero
                    work[i, p, k, r : r + 8, :] = zero

    def clear(first):
        @pl.loop(0, PANELS + 2)
        def _(k):
            for i in range(2):
                for p in range(2):
                    for r in range(0, rows, 8):
                        field[i, p, k, pad + first + r : pad + first + r + 8, :] = zero

        @pl.loop(0, secs)
        def _(s):
            for k in range(PANELS):
                for r in range(0, rows, 8):
                    index[s, k, first + r : first + r + 8, :] = zero

    @pl.when(jnp.logical_not(has_up))
    def _():
        clear(0)

    @pl.when(jnp.logical_not(has_down))
    def _():
        clear(2 * rows)

    for r in range(0, ext, 8):
        place = lax.broadcasted_iota(jnp.int32, (8, LANES), 0) + (t * rows + r - rows)
        inside = jnp.logical_and(place >= 0, place < tiles * rows)
        for i, c in enumerate(SCALES):
            scale[i, r : r + 8, :] = jnp.where(inside, jnp.float32(c), jnp.float32(0.0))

    edges(me)
    arrived(sid(3, 0))
    send(sid(3, 0), halves[0], sid(1, 0))
    arrived(sid(1, 0))
    send(sid(1, 0), halves[1], sid(3, 0))
    for da in (3, 1):
        send(sid(da, 0), every, sid(0, 1))
        send(sid(da, 0), every, sid(0, 3))
        edges(sid(da, 0))
    arrived(sid(2, 0))
    send(sid(2, 0), every, sid(0, 1))
    send(sid(2, 0), every, sid(0, 3))
    edges(sid(2, 0))
    for da in (0, 3, 1, 2):
        arrived(sid(da, 3))
        send(sid(da, 3), halves[0], sid(0, 1))
        arrived(sid(da, 1))
        send(sid(da, 1), halves[1], sid(0, 3))
        edges(sid(da, 3))
        edges(sid(da, 1))
    for da in (0, 3, 1, 2):
        arrived(sid(da, 2))
        edges(sid(da, 2))

    groups = secs // GROUP

    @pl.loop(0, groups)
    def _(g):
        now, later = lax.rem(g, 2), lax.rem(g + 1, 2)
        cur, nxt = field.at[now], field.at[later]
        both_in(lambda side: field_copy(now, side), lambda c: c.wait_recv())
        both(lambda side: field_copy(now, side), lambda c: c.wait_send())
        ghosts(cur, [blk for blk in range(ext // 8) if not rows <= 8 * blk < 2 * rows])
        for j in range(GROUP):
            s = g * GROUP + j
            both_in(lambda side: index_copy(s, depth_of(j), side), lambda c: c.wait_recv())
            for i in range(4):
                n = 4 * j + i + 1
                first, last = n // 8, -(-(ext - n) // 8)
                src = cur if i == 0 else work.at[(i + 1) % 2]
                dst = work.at[i % 2] if i < 3 else (cur if j < GROUP - 1 else nxt)
                stage(src, dst, cur, s, i, first, last)

        @pl.when(g < groups - 1)
        def _():
            both(lambda side: field_copy(later, side), lambda c: c.start())

    final = field.at[groups % 2]
    for p in range(2):
        for r in range(0, rows, 8):
            f = [final[p, k + 1, pad + rows + r : pad + rows + r + 8, :] for k in range(PANELS)]
            for k, v in enumerate(swap_bits(f)):
                out[0, p, r : r + 8, k * LANES : (k + 1) * LANES] = v

    for copy in sends:
        copy.wait_send()
    for s in range(secs):
        both(lambda side, s=s: index_copy(s, depth_of(s % GROUP), side), lambda c: c.wait_send())


def per_device(tiles, secs, beams, medium):
    rows = medium.shape[1]
    vmem = pl.BlockSpec(memory_space=pltpu.VMEM)
    return pl.pallas_call(
        functools.partial(kernel, tiles, secs),
        out_shape=jax.ShapeDtypeStruct(beams.shape, jnp.float32),
        in_specs=[vmem, vmem],
        out_specs=vmem,
        scratch_shapes=[
            pltpu.VMEM((2, 2, PANELS + 2, 3 * rows + 16, LANES), jnp.float32),
            pltpu.VMEM((2, 2, PANELS + 2, 3 * rows + 16, LANES), jnp.float32),
            pltpu.VMEM((secs, PANELS, 3 * rows, LANES), jnp.float32),
            pltpu.VMEM((4, 3 * rows, LANES), jnp.float32),
            pltpu.SemaphoreType.DMA((20,)),
            pltpu.SemaphoreType.DMA((secs,)),
            pltpu.SemaphoreType.DMA((secs, 2)),
            pltpu.SemaphoreType.DMA((secs, 2)),
            pltpu.SemaphoreType.DMA((2, 2)),
            pltpu.SemaphoreType.DMA((2, 2)),
        ],
        compiler_params=pltpu.CompilerParams(collective_id=0, has_side_effects=True),
        name="propagate",
    )(beams, medium)


def solution(mesh):
    placed = (P("sec", None, "tile", None), P("sec", "tile", None))
    return jax.shard_map(
        functools.partial(per_device, mesh.shape["tile"], mesh.shape["sec"]),
        mesh=mesh,
        in_specs=placed,
        out_specs=P("sec", None, "tile", None),
        check_vma=False,
    )
```

```python
import functools

import jax
import jax.numpy as jnp
from jax import lax
from jax.experimental import pallas as pl
from jax.experimental.pallas import tpu as pltpu
from jax.sharding import PartitionSpec as P

MESH = pl.DeviceIdType.MESH
STEP = 0.65
DIFFRACT = 0.5
SCALES = tuple(DIFFRACT * STEP / d for d in (4.0, 3.0, 2.0, 1.0))
GROUP = 4
PANELS = 16
LANES = 128
UNROLL = 4


def swap_bits(tiles):
    lane = lax.broadcasted_iota(jnp.int32, tiles[0].shape, len(tiles[0].shape) - 1)
    axis = len(tiles[0].shape) - 1
    tiles = list(tiles)
    for bit in range(4):
        low = (lane & (1 << bit)) == 0
        for i in range(PANELS):
            if i & (1 << bit):
                continue
            j = i | (1 << bit)
            x, y = tiles[i], tiles[j]
            tiles[i] = jnp.where(low, x, pltpu.roll(y, 1 << bit, axis))
            tiles[j] = jnp.where(low, pltpu.roll(x, LANES - (1 << bit), axis), y)
    return tiles


def kernel(tiles, secs, beams, medium, out, field, work_a, work_b, index, scale, m_send, m_recv, h_send, h_recv, f_send, f_recv):
    rows = medium.shape[1]
    ext = 3 * rows
    pad = 8
    me = lax.axis_index("sec")
    t = lax.axis_index("tile")
    odd = lax.rem(t, 2)
    y, x = lax.div(me, 4), lax.rem(me, 4)
    a = x * (1 - odd) + y * odd
    b = y * (1 - odd) + x * odd

    def sid(da, db):
        return lax.rem(a + da, 4) * (1 + 3 * odd) + lax.rem(b + db, 4) * (4 - 3 * odd)

    has_up = t > 0
    has_down = t < tiles - 1

    barrier = pltpu.get_barrier_semaphore()
    for peer in (sid(1, 0), sid(3, 0), sid(0, 1), sid(0, 3)):
        pl.semaphore_signal(barrier, inc=1, device_id=(peer, t), device_id_type=MESH)

    @pl.when(has_up)
    def _():
        pl.semaphore_signal(barrier, inc=1, device_id=(me, t - 1), device_id_type=MESH)

    @pl.when(has_down)
    def _():
        pl.semaphore_signal(barrier, inc=1, device_id=(me, t + 1), device_id_type=MESH)

    def field_copy(buf, side):
        mine = field.at[buf, :, 1 : PANELS + 1, pad + rows : pad + 2 * rows, :]
        first = pad + (2 * rows if side == 0 else 0)
        theirs = field.at[buf, :, 1 : PANELS + 1, first : first + rows, :]
        return pltpu.make_async_remote_copy(
            src_ref=mine, dst_ref=theirs, send_sem=f_send.at[buf, side], recv_sem=f_recv.at[buf, side],
            device_id=(me, t - 1 if side == 0 else t + 1), device_id_type=MESH)

    def index_copy(s, depth, side):
        first = rows if side == 0 else 2 * rows - depth
        there = 2 * rows if side == 0 else rows - depth
        return pltpu.make_async_remote_copy(
            src_ref=index.at[s, :, first : first + depth, :], dst_ref=index.at[s, :, there : there + depth, :],
            send_sem=h_send.at[s, side], recv_sem=h_recv.at[s, side],
            device_id=(me, t - 1 if side == 0 else t + 1), device_id_type=MESH)

    def both(make, act):
        @pl.when(has_up)
        def _():
            act(make(0))

        @pl.when(has_down)
        def _():
            act(make(1))

    def both_in(make, act):
        @pl.when(has_down)
        def _():
            act(make(0))

        @pl.when(has_up)
        def _():
            act(make(1))

    def depth_of(j):
        return rows - 4 * j

    sends = []
    halves = (pl.ds(0, PANELS // 2), pl.ds(PANELS // 2, PANELS // 2))
    every = pl.ds(0, PANELS)

    def send(s, part, peer):
        ref = index.at[s, part, rows : 2 * rows, :]
        copy = pltpu.make_async_remote_copy(
            src_ref=ref, dst_ref=ref, send_sem=m_send.at[len(sends)], recv_sem=m_recv.at[s],
            device_id=(peer, t), device_id_type=MESH)
        copy.start()
        sends.append(copy)

    def edges(s):
        for j in range(GROUP):
            @pl.when(lax.rem(s, GROUP) == j)
            def _():
                both(lambda side: index_copy(s, depth_of(j), side), lambda c: c.start())

    def first_edges(s):
        for j in range(GROUP):
            @pl.when(s == j)
            def _():
                both(lambda side: index_copy(j, depth_of(j), side), lambda c: c.start())

    def later_edges(g):
        for j in range(GROUP):
            @pl.when(g * (1 - odd) + j * odd != b)
            def _():
                both(lambda side: index_copy(g * GROUP + j, depth_of(j), side), lambda c: c.start())

    def arrived(s):
        ref = index.at[s, :, rows : 2 * rows, :]
        pltpu.make_async_remote_copy(
            src_ref=ref, dst_ref=ref, send_sem=m_send.at[0], recv_sem=m_recv.at[s],
            device_id=(me, t), device_id_type=MESH).wait_recv()

    for r in range(0, rows, 8):
        m = [2.0 * medium[0, r : r + 8, k * LANES : (k + 1) * LANES] - 4.0 for k in range(PANELS)]
        for k, v in enumerate(swap_bits(m)):
            index[me, k, rows + r : rows + r + 8, :] = v
    pl.semaphore_wait(barrier, 4 + has_up.astype(jnp.int32) + has_down.astype(jnp.int32))
    send(me, every, sid(1, 0))
    send(me, every, sid(3, 0))
    send(me, every, sid(0, 1))
    send(me, every, sid(0, 3))
    for p in range(2):
        for r in range(0, rows, 8):
            f = [beams[0, p, r : r + 8, k * LANES : (k + 1) * LANES] for k in range(PANELS)]
            for k, v in enumerate(swap_bits(f)):
                field[0, p, k + 1, pad + rows + r : pad + rows + r + 8, :] = v

    both(lambda side: field_copy(0, side), lambda c: c.start())
    lane = lax.broadcasted_iota(jnp.int32, (8, LANES), 1)

    def before_first(v):
        left = jnp.where(lane < 16, pltpu.roll(v, 17, 1), pltpu.roll(v, 16, 1))
        return jnp.where(lane == 0, 0.0, left)

    def after_last(v):
        right = jnp.where(lane >= LANES - 16, pltpu.roll(v, LANES - 17, 1), pltpu.roll(v, LANES - 16, 1))
        return jnp.where(lane == LANES - 1, 0.0, right)

    def ghosts(ref, blocks):
        for blk in blocks:
            for p in range(2):
                r = pad + 8 * blk
                ref[p, 0, r : r + 8, :] = before_first(ref[p, PANELS, r : r + 8, :])
                ref[p, PANELS + 1, r : r + 8, :] = after_last(ref[p, 1, r : r + 8, :])

    def stage(src, dst, base, s, i, first, last):
        for k0 in (PANELS - UNROLL,) + tuple(range(0, PANELS - UNROLL, UNROLL)):
            for blk in range(first, last):
                r = pad + 8 * blk
                w = scale[i, 8 * blk : 8 * blk + 8, :]
                mid = [[src[p, k0 + q, r : r + 8, :] for q in range(UNROLL + 2)] for p in range(2)]
                for u in range(UNROLL):
                    k = k0 + u
                    m = index[s, k, 8 * blk : 8 * blk + 8, :]
                    drive = []
                    for p in range(2):
                        rowsum = src[p, k + 1, r - 1 : r + 7, :] + src[p, k + 1, r + 1 : r + 9, :]
                        drive.append(((mid[p][u] + mid[p][u + 2]) + rowsum + m * mid[p][u + 1]) * w)
                    new = (base[0, k + 1, r : r + 8, :] - drive[1], base[1, k + 1, r : r + 8, :] + drive[0])
                    for p in range(2):
                        dst[p, k + 1, r : r + 8, :] = new[p]
                        if k == 0:
                            dst[p, PANELS + 1, r : r + 8, :] = after_last(new[p])
                        if k == PANELS - 1:
                            dst[p, 0, r : r + 8, :] = before_first(new[p])

    ghosts(field.at[0], range(rows // 8, 2 * rows // 8))
    zero = jnp.zeros((8, LANES), jnp.float32)

    @pl.loop(0, PANELS + 2)
    def _(k):
        for i in range(2):
            for p in range(2):
                for r in (0, pad + ext):
                    field[i, p, k, r : r + 8, :] = zero
                    (work_a, work_b)[i][p, k, r : r + 8, :] = zero

    def clear(first):
        @pl.loop(0, PANELS + 2)
        def _(k):
            for i in range(2):
                for p in range(2):
                    for r in range(0, rows, 8):
                        field[i, p, k, pad + first + r : pad + first + r + 8, :] = zero

        @pl.loop(0, secs)
        def _(s):
            for k in range(PANELS):
                for r in range(0, rows, 8):
                    index[s, k, first + r : first + r + 8, :] = zero

    @pl.when(jnp.logical_not(has_up))
    def _():
        clear(0)

    @pl.when(jnp.logical_not(has_down))
    def _():
        clear(2 * rows)

    for r in range(0, ext, 8):
        place = lax.broadcasted_iota(jnp.int32, (8, LANES), 0) + (t * rows + r - rows)
        inside = jnp.logical_and(place >= 0, place < tiles * rows)
        for i, c in enumerate(SCALES):
            scale[i, r : r + 8, :] = jnp.where(inside, jnp.float32(c), jnp.float32(0.0))

    edges(me)
    arrived(sid(3, 0))
    send(sid(3, 0), halves[0], sid(1, 0))
    arrived(sid(1, 0))
    send(sid(1, 0), halves[1], sid(3, 0))
    for da in (3, 1):
        send(sid(da, 0), every, sid(0, 1))
        send(sid(da, 0), every, sid(0, 3))
        edges(sid(da, 0))
    arrived(sid(2, 0))
    send(sid(2, 0), every, sid(0, 1))
    send(sid(2, 0), every, sid(0, 3))
    edges(sid(2, 0))
    for da in (0, 3, 1, 2):
        arrived(sid(da, 3))
        send(sid(da, 3), halves[0], sid(0, 1))
        arrived(sid(da, 1))
        send(sid(da, 1), halves[1], sid(0, 3))
        first_edges(sid(da, 3))
        first_edges(sid(da, 1))
    for da in (0, 3, 1, 2):
        arrived(sid(da, 2))
        first_edges(sid(da, 2))

    groups = secs // GROUP

    @pl.loop(0, groups)
    def _(g):
        now, later = lax.rem(g, 2), lax.rem(g + 1, 2)
        cur, nxt = field.at[now], field.at[later]
        both_in(lambda side: field_copy(now, side), lambda c: c.wait_recv())
        both(lambda side: field_copy(now, side), lambda c: c.wait_send())

        @pl.when(g < groups - 1)
        def _():
            later_edges(g + 1)

        ghosts(cur, [blk for blk in range(ext // 8) if not rows <= 8 * blk < 2 * rows])
        for j in range(GROUP):
            s = g * GROUP + j
            both_in(lambda side: index_copy(s, depth_of(j), side), lambda c: c.wait_recv())
            for i in range(4):
                n = 4 * j + i + 1
                first, last = n // 8, -(-(ext - n) // 8)
                src = cur if i == 0 else (work_a, work_b)[(i + 1) % 2]
                dst = (work_a, work_b)[i % 2] if i < 3 else (cur if j < GROUP - 1 else nxt)
                stage(src, dst, cur, s, i, first, last)

        @pl.when(g < groups - 1)
        def _():
            both(lambda side: field_copy(later, side), lambda c: c.start())

    final = field.at[groups % 2]
    for p in range(2):
        for r in range(0, rows, 8):
            f = [final[p, k + 1, pad + rows + r : pad + rows + r + 8, :] for k in range(PANELS)]
            for k, v in enumerate(swap_bits(f)):
                out[0, p, r : r + 8, k * LANES : (k + 1) * LANES] = v

    for copy in sends:
        copy.wait_send()
    for s in range(secs):
        both(lambda side, s=s: index_copy(s, depth_of(s % GROUP), side), lambda c: c.wait_send())


def per_device(tiles, secs, beams, medium):
    rows = medium.shape[1]
    vmem = pl.BlockSpec(memory_space=pltpu.VMEM)
    return pl.pallas_call(
        functools.partial(kernel, tiles, secs),
        out_shape=jax.ShapeDtypeStruct(beams.shape, jnp.float32),
        in_specs=[vmem, vmem],
        out_specs=vmem,
        scratch_shapes=[
            pltpu.VMEM((2, 2, PANELS + 2, 3 * rows + 16, LANES), jnp.float32),
            pltpu.VMEM((2, PANELS + 2, 3 * rows + 16, LANES), jnp.float32),
            pltpu.VMEM((2, PANELS + 2, 3 * rows + 16, LANES), jnp.float32),
            pltpu.VMEM((secs, PANELS, 3 * rows, LANES), jnp.float32),
            pltpu.VMEM((4, 3 * rows, LANES), jnp.float32),
            pltpu.SemaphoreType.DMA((20,)),
            pltpu.SemaphoreType.DMA((secs,)),
            pltpu.SemaphoreType.DMA((secs, 2)),
            pltpu.SemaphoreType.DMA((secs, 2)),
            pltpu.SemaphoreType.DMA((2, 2)),
            pltpu.SemaphoreType.DMA((2, 2)),
        ],
        compiler_params=pltpu.CompilerParams(collective_id=0, has_side_effects=True),
        name="propagate",
    )(beams, medium)


def solution(mesh):
    placed = (P("sec", None, "tile", None), P("sec", "tile", None))
    return jax.shard_map(
        functools.partial(per_device, mesh.shape["tile"], mesh.shape["sec"]),
        mesh=mesh,
        in_specs=placed,
        out_specs=P("sec", None, "tile", None),
        check_vma=False,
    )
```

```python
import functools

import jax
import jax.numpy as jnp
from jax import lax
from jax.experimental import pallas as pl
from jax.experimental.pallas import tpu as pltpu
from jax.sharding import PartitionSpec as P

MESH = pl.DeviceIdType.MESH
STEP = 0.65
DIFFRACT = 0.5
SCALES = tuple(DIFFRACT * STEP / d for d in (4.0, 3.0, 2.0, 1.0))
GROUP = 4
PANELS = 16
LANES = 128
UNROLL = 4


def swap_bits(tiles):
    lane = lax.broadcasted_iota(jnp.int32, tiles[0].shape, len(tiles[0].shape) - 1)
    axis = len(tiles[0].shape) - 1
    tiles = list(tiles)
    for bit in range(4):
        low = (lane & (1 << bit)) == 0
        for i in range(PANELS):
            if i & (1 << bit):
                continue
            j = i | (1 << bit)
            x, y = tiles[i], tiles[j]
            tiles[i] = jnp.where(low, x, pltpu.roll(y, 1 << bit, axis))
            tiles[j] = jnp.where(low, pltpu.roll(x, LANES - (1 << bit), axis), y)
    return tiles


def kernel(tiles, secs, beams, medium, out, field, work_a, work_b, index, scale, m_send, m_recv, h_send, h_recv, f_send, f_recv):
    rows = medium.shape[1]
    ext = 3 * rows
    pad = 8
    me = lax.axis_index("sec")
    t = lax.axis_index("tile")
    odd = lax.rem(t, 2)
    y, x = lax.div(me, 4), lax.rem(me, 4)
    a = x * (1 - odd) + y * odd
    b = y * (1 - odd) + x * odd

    def sid(da, db):
        return lax.rem(a + da, 4) * (1 + 3 * odd) + lax.rem(b + db, 4) * (4 - 3 * odd)

    has_up = t > 0
    has_down = t < tiles - 1

    barrier = pltpu.get_barrier_semaphore()
    for peer in (sid(1, 0), sid(3, 0), sid(0, 1), sid(0, 3)):
        pl.semaphore_signal(barrier, inc=1, device_id=(peer, t), device_id_type=MESH)

    @pl.when(has_up)
    def _():
        pl.semaphore_signal(barrier, inc=1, device_id=(me, t - 1), device_id_type=MESH)

    @pl.when(has_down)
    def _():
        pl.semaphore_signal(barrier, inc=1, device_id=(me, t + 1), device_id_type=MESH)

    def field_copy(buf, side):
        mine = field.at[buf, :, 1 : PANELS + 1, pad + rows : pad + 2 * rows, :]
        first = pad + (2 * rows if side == 0 else 0)
        theirs = field.at[buf, :, 1 : PANELS + 1, first : first + rows, :]
        return pltpu.make_async_remote_copy(
            src_ref=mine, dst_ref=theirs, send_sem=f_send.at[buf, side], recv_sem=f_recv.at[buf, side],
            device_id=(me, t - 1 if side == 0 else t + 1), device_id_type=MESH)

    def index_copy(s, depth, side):
        first = rows if side == 0 else 2 * rows - depth
        there = 2 * rows if side == 0 else rows - depth
        return pltpu.make_async_remote_copy(
            src_ref=index.at[s, :, first : first + depth, :], dst_ref=index.at[s, :, there : there + depth, :],
            send_sem=h_send.at[s, side], recv_sem=h_recv.at[s, side],
            device_id=(me, t - 1 if side == 0 else t + 1), device_id_type=MESH)

    def both(make, act):
        @pl.when(has_up)
        def _():
            act(make(0))

        @pl.when(has_down)
        def _():
            act(make(1))

    def both_in(make, act):
        @pl.when(has_down)
        def _():
            act(make(0))

        @pl.when(has_up)
        def _():
            act(make(1))

    def depth_of(j):
        return rows - 4 * j

    sends = []
    halves = (pl.ds(0, PANELS // 2), pl.ds(PANELS // 2, PANELS // 2))
    every = pl.ds(0, PANELS)

    def send(s, part, peer):
        ref = index.at[s, part, rows : 2 * rows, :]
        copy = pltpu.make_async_remote_copy(
            src_ref=ref, dst_ref=ref, send_sem=m_send.at[len(sends)], recv_sem=m_recv.at[s],
            device_id=(peer, t), device_id_type=MESH)
        copy.start()
        sends.append(copy)

    def edges(s):
        for j in range(GROUP):
            @pl.when(lax.rem(s, GROUP) == j)
            def _():
                both(lambda side: index_copy(s, depth_of(j), side), lambda c: c.start())

    def first_edges(s):
        @pl.when(s < GROUP)
        def _():
            for j in range(GROUP):
                @pl.when(s == j)
                def _():
                    both(lambda side: index_copy(j, depth_of(j), side), lambda c: c.start())

    def later_edges(g):
        for j in range(GROUP):
            @pl.when(g * (1 - odd) + j * odd != b)
            def _():
                both(lambda side: index_copy(g * GROUP + j, depth_of(j), side), lambda c: c.start())

    def arrived(s):
        ref = index.at[s, :, rows : 2 * rows, :]
        pltpu.make_async_remote_copy(
            src_ref=ref, dst_ref=ref, send_sem=m_send.at[0], recv_sem=m_recv.at[s],
            device_id=(me, t), device_id_type=MESH).wait_recv()

    for r in range(0, rows, 8):
        m = [2.0 * medium[0, r : r + 8, k * LANES : (k + 1) * LANES] - 4.0 for k in range(PANELS)]
        for k, v in enumerate(swap_bits(m)):
            index[me, k, rows + r : rows + r + 8, :] = v
    pl.semaphore_wait(barrier, 4 + has_up.astype(jnp.int32) + has_down.astype(jnp.int32))
    send(me, every, sid(1, 0))
    send(me, every, sid(3, 0))
    send(me, every, sid(0, 1))
    send(me, every, sid(0, 3))
    for p in range(2):
        for r in range(0, rows, 8):
            f = [beams[0, p, r : r + 8, k * LANES : (k + 1) * LANES] for k in range(PANELS)]
            for k, v in enumerate(swap_bits(f)):
                field[0, p, k + 1, pad + rows + r : pad + rows + r + 8, :] = v

    both(lambda side: field_copy(0, side), lambda c: c.start())
    lane = lax.broadcasted_iota(jnp.int32, (8, LANES), 1)

    def before_first(v):
        left = jnp.where(lane < 16, pltpu.roll(v, 17, 1), pltpu.roll(v, 16, 1))
        return jnp.where(lane == 0, 0.0, left)

    def after_last(v):
        right = jnp.where(lane >= LANES - 16, pltpu.roll(v, LANES - 17, 1), pltpu.roll(v, LANES - 16, 1))
        return jnp.where(lane == LANES - 1, 0.0, right)

    def ghosts(ref, blocks):
        for blk in blocks:
            for p in range(2):
                r = pad + 8 * blk
                ref[p, 0, r : r + 8, :] = before_first(ref[p, PANELS, r : r + 8, :])
                ref[p, PANELS + 1, r : r + 8, :] = after_last(ref[p, 1, r : r + 8, :])

    def stage(src, dst, base, s, i, first, last):
        ends = (PANELS - UNROLL, 0)
        inner = tuple(range(UNROLL, PANELS - UNROLL, UNROLL))
        for k0 in (inner + ends if i == 0 and first == 0 and base is src else ends + inner):
            for blk in range(first, last):
                r = pad + 8 * blk
                w = scale[i, 8 * blk : 8 * blk + 8, :]
                mid = [[src[p, k0 + q, r : r + 8, :] for q in range(UNROLL + 2)] for p in range(2)]
                for u in range(UNROLL):
                    k = k0 + u
                    m = index[s, k, 8 * blk : 8 * blk + 8, :]
                    drive = []
                    for p in range(2):
                        rowsum = src[p, k + 1, r - 1 : r + 7, :] + src[p, k + 1, r + 1 : r + 9, :]
                        drive.append(((mid[p][u] + mid[p][u + 2]) + rowsum + m * mid[p][u + 1]) * w)
                    new = (base[0, k + 1, r : r + 8, :] - drive[1], base[1, k + 1, r : r + 8, :] + drive[0])
                    for p in range(2):
                        dst[p, k + 1, r : r + 8, :] = new[p]
                        if k == 0:
                            dst[p, PANELS + 1, r : r + 8, :] = after_last(new[p])
                        if k == PANELS - 1:
                            dst[p, 0, r : r + 8, :] = before_first(new[p])

    ghosts(field.at[0], range(rows // 8, 2 * rows // 8))
    zero = jnp.zeros((8, LANES), jnp.float32)

    @pl.loop(0, PANELS + 2)
    def _(k):
        for i in range(2):
            for p in range(2):
                for r in (0, pad + ext):
                    field[i, p, k, r : r + 8, :] = zero
                    (work_a, work_b)[i][p, k, r : r + 8, :] = zero

    def clear(first):
        @pl.loop(0, PANELS + 2)
        def _(k):
            for i in range(2):
                for p in range(2):
                    for r in range(0, rows, 8):
                        field[i, p, k, pad + first + r : pad + first + r + 8, :] = zero

        @pl.loop(0, secs)
        def _(s):
            for k in range(PANELS):
                for r in range(0, rows, 8):
                    index[s, k, first + r : first + r + 8, :] = zero

    @pl.when(jnp.logical_not(has_up))
    def _():
        clear(0)

    @pl.when(jnp.logical_not(has_down))
    def _():
        clear(2 * rows)

    for r in range(0, ext, 8):
        place = lax.broadcasted_iota(jnp.int32, (8, LANES), 0) + (t * rows + r - rows)
        inside = jnp.logical_and(place >= 0, place < tiles * rows)
        for i, c in enumerate(SCALES):
            scale[i, r : r + 8, :] = jnp.where(inside, jnp.float32(c), jnp.float32(0.0))

    edges(me)
    arrived(sid(3, 0))
    send(sid(3, 0), halves[0], sid(1, 0))
    arrived(sid(1, 0))
    send(sid(1, 0), halves[1], sid(3, 0))
    for da in (3, 1):
        send(sid(da, 0), every, sid(0, 1))
        send(sid(da, 0), every, sid(0, 3))
        edges(sid(da, 0))

    def relay(da):
        arrived(sid(da, 3))
        send(sid(da, 3), halves[0], sid(0, 1))
        arrived(sid(da, 1))
        send(sid(da, 1), halves[1], sid(0, 3))
        first_edges(sid(da, 3))
        first_edges(sid(da, 1))

    relay(0)
    arrived(sid(2, 0))
    send(sid(2, 0), every, sid(0, 1))
    send(sid(2, 0), every, sid(0, 3))
    edges(sid(2, 0))
    for da in (3, 1, 2):
        relay(da)
    for da in (0, 3, 1, 2):
        arrived(sid(da, 2))
        first_edges(sid(da, 2))

    groups = secs // GROUP

    @pl.loop(0, groups)
    def _(g):
        now, later = lax.rem(g, 2), lax.rem(g + 1, 2)
        cur, nxt = field.at[now], field.at[later]
        both_in(lambda side: field_copy(now, side), lambda c: c.wait_recv())
        both(lambda side: field_copy(now, side), lambda c: c.wait_send())
        for j in range(GROUP):
            s = g * GROUP + j
            both_in(lambda side: index_copy(s, depth_of(j), side), lambda c: c.wait_recv())
            if j == 0:
                @pl.when(g == 0)
                def _():
                    later_edges(1)
                ghosts(cur, [blk for blk in range(ext // 8) if not rows <= 8 * blk < 2 * rows])
            for i in range(4):
                n = 4 * j + i + 1
                first, last = n // 8, -(-(ext - n) // 8)
                src = cur if i == 0 else (work_a, work_b)[(i + 1) % 2]
                dst = (work_a, work_b)[i % 2] if i < 3 else (cur if j < GROUP - 1 else nxt)
                stage(src, dst, cur, s, i, first, last)

        @pl.when(g < groups - 1)
        def _():
            both(lambda side: field_copy(later, side), lambda c: c.start())

            @pl.when(g < groups - 2)
            def _():
                later_edges(g + 2)

            @pl.when(g == 0)
            def _():
                for copy in sends:
                    copy.wait_send()

            for j in range(GROUP):
                both(lambda side: index_copy(g * GROUP + j, depth_of(j), side), lambda c: c.wait_send())

    final = field.at[groups % 2]
    for p in range(2):
        for r in range(0, rows, 8):
            f = [final[p, k + 1, pad + rows + r : pad + rows + r + 8, :] for k in range(PANELS)]
            for k, v in enumerate(swap_bits(f)):
                out[0, p, r : r + 8, k * LANES : (k + 1) * LANES] = v

    for s in range(secs - GROUP, secs):
        both(lambda side, s=s: index_copy(s, depth_of(s % GROUP), side), lambda c: c.wait_send())


def per_device(tiles, secs, beams, medium):
    rows = medium.shape[1]
    vmem = pl.BlockSpec(memory_space=pltpu.VMEM)
    return pl.pallas_call(
        functools.partial(kernel, tiles, secs),
        out_shape=jax.ShapeDtypeStruct(beams.shape, jnp.float32),
        in_specs=[vmem, vmem],
        out_specs=vmem,
        scratch_shapes=[
            pltpu.VMEM((2, 2, PANELS + 2, 3 * rows + 16, LANES), jnp.float32),
            pltpu.VMEM((2, PANELS + 2, 3 * rows + 16, LANES), jnp.float32),
            pltpu.VMEM((2, PANELS + 2, 3 * rows + 16, LANES), jnp.float32),
            pltpu.VMEM((secs, PANELS, 3 * rows, LANES), jnp.float32),
            pltpu.VMEM((4, 3 * rows, LANES), jnp.float32),
            pltpu.SemaphoreType.DMA((20,)),
            pltpu.SemaphoreType.DMA((secs,)),
            pltpu.SemaphoreType.DMA((secs, 2)),
            pltpu.SemaphoreType.DMA((secs, 2)),
            pltpu.SemaphoreType.DMA((2, 2)),
            pltpu.SemaphoreType.DMA((2, 2)),
        ],
        compiler_params=pltpu.CompilerParams(collective_id=0, has_side_effects=True),
        name="propagate",
    )(beams, medium)


def solution(mesh):
    placed = (P("sec", None, "tile", None), P("sec", "tile", None))
    return jax.shard_map(
        functools.partial(per_device, mesh.shape["tile"], mesh.shape["sec"]),
        mesh=mesh,
        in_specs=placed,
        out_specs=P("sec", None, "tile", None),
        check_vma=False,
    )
```
